32 devices in a mesh: slot: 4 (over y, x), feat: 8 (over z, core).
Axes of the slice: x: 2, y: 2, z: 4, core: 2. Of those that a mesh axis runs over, the one named last changes fastest.
Arguments:
- acts_in: bfloat16 [3, 256, 2304], P(None, None, 'slot'), may hold values from -6 to 6
- acts_out: bfloat16 [3, 256, 2304], P(None, None, 'slot'), may hold values from -6 to 6
- enc_weight: bfloat16 [3, 2304, 16384], P(None, 'slot', 'feat'), may hold values from -0.125 to 0.125
- enc_bias: float32 [3, 16384], P(None, 'feat'), may hold values from -3 to 3
- dec_weight: bfloat16 [6, 16384, 2304], P(None, 'feat', 'slot'), may hold values from -0.046875 to 0.046875
- dec_bias: float32 [3, 2304], P(None, 'slot'), may hold values from -3 to 3
Outputs:
- enc_grad: float32 [3, 2304, 16384], P(None, 'slot', 'feat')
- enc_bias_grad: float32 [3, 16384], P(None, 'feat')
- dec_grad: float32 [6, 16384, 2304], P(None, 'feat', 'slot')
- mse: float32 [], replicated
The draws below stay inside these ranges and needn't reach their ends.
All inputs are finite; a program needn't handle non-finite values.
Results may differ from the reference program's by a relative error of at most 0.0095.
Values may be sent and summed in bfloat16 or wider, within the bound.
A program may use at most 128 MiB of HBM per device.

```python
import jax
import jax.numpy as jnp
from jax import lax

D = 2304
F = 16384
L = 3
TOKENS = 256
PAIRS = 6


def block_scale(own_key, shape, split, smallest, high):
    factor_of = 1.0
    for axis_at, shards_of in split:
        steps = jax.random.uniform(jax.random.fold_in(jax.random.fold_in(own_key, 6), axis_at), (shards_of,), jnp.float32, smallest / len(split), high / len(split))
        factor_of = factor_of * jnp.repeat(jnp.exp(steps), shape[axis_at] // shards_of).reshape((-1,) + (1,) * (len(shape) - 1 - axis_at))
    return factor_of


def scatter_about(rng, dims, spread, most, cuts=(), kind=jnp.bfloat16):
    entries = spread * jax.random.normal(rng, dims, jnp.float32)
    if cuts:
        entries = entries * block_scale(rng, dims, cuts, -0.22, 0.18)
    return jnp.clip(entries, -most, most).astype(kind)


def setup_inputs(seed: int = 0) -> dict:
    key_list = jax.random.split(jax.random.key(seed), 7)
    return {
        "acts_in": scatter_about(key_list[0], (L, TOKENS, D), 1.0, 6.0, ((2, 4),)),
        "acts_out": scatter_about(key_list[1], (L, TOKENS, D), 1.0, 6.0, ((2, 4),)),
        "enc_weight": scatter_about(key_list[2], (L, D, F), D ** -0.5, 0.125, ((1, 4), (2, 8))),
        "enc_bias": scatter_about(key_list[3], (L, F), 0.5, 3.0, ((1, 8),), jnp.float32),
        "dec_weight": scatter_about(key_list[4], (PAIRS, F, D), F ** -0.5, 0.046875, ((1, 8), (2, 4))),
        "dec_bias": scatter_about(key_list[5], (L, D), 0.5, 3.0, ((1, 4),), jnp.float32),
    }


def pair_number(src_layer, dst_layer):
    return src_layer * L - src_layer * (src_layer - 1) // 2 + (dst_layer - src_layer)


def reference(acts_in, acts_out, enc_weight, enc_bias, dec_weight, dec_bias):
    features = []
    slopes = []
    for src_layer in range(L):
        preact = jnp.dot(acts_in[src_layer], enc_weight[src_layer], preferred_element_type=jnp.float32) + enc_bias[src_layer]
        features.append(jnp.maximum(preact, 0.0).astype(jnp.bfloat16))
        slopes.append(jnp.where(preact > 0, 1.0, 0.0).astype(jnp.bfloat16))
    errors = []
    squared = jnp.zeros((), jnp.float32)
    for dst_layer in range(L):
        rebuilt = jnp.zeros((TOKENS, D), jnp.float32)
        for src_layer in range(dst_layer + 1):
            rebuilt = rebuilt + jnp.dot(features[src_layer], dec_weight[pair_number(src_layer, dst_layer)], preferred_element_type=jnp.float32)
        error_full = rebuilt + dec_bias[dst_layer] - acts_out[dst_layer].astype(jnp.float32)
        squared = squared + jnp.sum(error_full * error_full)
        errors.append(error_full.astype(jnp.bfloat16))
    mse = squared / (L * TOKENS * D)
    dec_grads = []
    for src_layer in range(L):
        for dst_layer in range(src_layer, L):
            dec_grads.append(lax.dot_general(features[src_layer], errors[dst_layer], (((0,), (0,)), ((), ())), preferred_element_type=jnp.float32))
    enc_grads = []
    bias_grads = []
    for src_layer in range(L):
        upstream = jnp.zeros((TOKENS, F), jnp.float32)
        for dst_layer in range(src_layer, L):
            upstream = upstream + lax.dot_general(errors[dst_layer], dec_weight[pair_number(src_layer, dst_layer)], (((1,), (1,)), ((), ())), preferred_element_type=jnp.float32)
        delta = upstream * slopes[src_layer].astype(jnp.float32)
        bias_grads.append(jnp.sum(delta, axis=0))
        enc_grads.append(lax.dot_general(acts_in[src_layer], delta.astype(jnp.bfloat16), (((0,), (0,)), ((), ())), preferred_element_type=jnp.float32))
    return jnp.stack(enc_grads), jnp.stack(bias_grads), jnp.stack(dec_grads), mse
```

```python
import functools

import jax
import jax.numpy as jnp
from jax import lax
from jax.experimental import pallas as pl
from jax.experimental.pallas import tpu as pltpu
from jax.sharding import PartitionSpec as P

MESH = pl.DeviceIdType.MESH
F32, BF16 = jnp.float32, jnp.bfloat16


def pairs_of(layers):
    return [(a, b) for a in range(layers) for b in range(a, layers)]


def bits_of(n_slot):
    bits = n_slot.bit_length() - 1
    assert 1 << bits == n_slot
    return bits


def step_kernel(
    n_slot, n_feat,
    acts, enc_hbm, enc_bias, dec_hbm, acts_out, dec_bias,
    feat_out, err_out, delta_out, sq_out,
    encw, decw, part, rxf, feat, acc, psend, prx, zsend, zrx, errw, errb, ub, rxu, delta, ms, mrx,
    local_sem, send_sem, recv_sem,
):
    layers, tokens, width = acts.shape
    fdev = encw.shape[2]
    half = tokens // 2
    groups = n_feat // 2
    rows = half // groups
    bits = bits_of(n_slot)
    pair_list = pairs_of(layers)
    n_pairs = len(pair_list)
    slot = lax.axis_index("slot")
    fidx = lax.axis_index("feat")
    core = fidx % 2
    zpos = fidx // 2
    bit = [(slot // (1 << i)) % 2 for i in range(bits)]
    across = [slot + (1 - 2 * bit[i]) * (1 << i) for i in range(bits)]
    partner = fidx + 1 - 2 * core
    zpeer = [((zpos + d) % groups) * 2 + core for d in range(groups)]

    n_local = [0]
    outs = []

    def local_copy(src, dst):
        c = pltpu.make_async_copy(src, dst, local_sem.at[n_local[0]])
        n_local[0] += 1
        c.start()
        return c

    enc_in = [local_copy(enc_hbm.at[s], encw.at[s]) for s in range(layers)]
    dec_in = [local_copy(dec_hbm.at[p], decw.at[p]) for p in range(n_pairs)]

    barrier = pltpu.get_barrier_semaphore()
    for i in range(bits):
        pl.semaphore_signal(barrier, inc=1, device_id={"slot": across[i]}, device_id_type=MESH)
    for peer in [partner] + zpeer[1:]:
        pl.semaphore_signal(barrier, inc=1, device_id={"feat": peer}, device_id_type=MESH)
    pl.semaphore_wait(barrier, bits + groups)

    n_remote = [0]
    unsent = []

    def send(src, dst, device):
        c = pltpu.make_async_remote_copy(
            src_ref=src, dst_ref=dst,
            send_sem=send_sem.at[n_remote[0]], recv_sem=recv_sem.at[n_remote[0]],
            device_id=device, device_id_type=MESH,
        )
        n_remote[0] += 1
        c.start()
        unsent.append(c)
        return c

    def drain():
        for c in unsent:
            c.wait_send()
        unsent.clear()

    orders = (list(range(bits)), list(range(bits))[::-1])

    def start_row(h, phase):
        at = h * half
        for j in range(phase):
            at = at + bit[orders[h][j]] * (half >> (j + 1))
        return at

    def block(h, phase):
        size = half >> phase
        at = start_row(h, phase)
        return pl.ds(pl.multiple_of(at, size) if phase else at, size)

    def other(h, phase):
        size = half >> (phase + 1)
        at = start_row(h, phase) + (1 - bit[orders[h][phase]]) * size
        return pl.ds(pl.multiple_of(at, size), size)

    def land(h, phase):
        return pl.ds(half - (half >> phase), half >> (phase + 1))

    def scatter_send(buf, rx, s, phase):
        return [
            send(buf.at[s, other(h, phase)], rx.at[s, h, land(h, phase)],
                 {"slot": across[orders[h][phase]]})
            for h in range(2)
        ]

    def gather_send(buf, s, phase):
        return [
            send(buf.at[s, block(h, phase + 1)], buf.at[s, block(h, phase + 1)],
                 {"slot": across[orders[h][phase]]})
            for h in range(2)
        ]

    def exchange(buf, rx, full, order, moving, finish, arrived):
        for phase in range(bits):
            following = {}
            for s in order:
                for h in range(2):
                    moving[s][h].wait_recv()
                    keep = block(h, phase + 1)
                    got = rx[s, h, land(h, phase)].astype(F32)
                    got = buf[s, keep].astype(F32) + got
                    if phase + 1 < bits:
                        buf[s, keep] = got.astype(buf.dtype)
                    else:
                        finish(s, keep, got)
                if phase + 1 < bits:
                    following[s] = scatter_send(buf, rx, s, phase + 1)
                else:
                    following[s] = gather_send(full, s, bits - 1)
            moving = following
        for phase in range(bits - 2, -1, -1):
            following = {}
            for s in order:
                for c in moving[s]:
                    c.wait_recv()
                following[s] = gather_send(full, s, phase)
            moving = following
        for s in order:
            for c in moving[s]:
                c.wait_recv()
            outs.append(arrived(s))

    tile = min(256, fdev)
    moving = {}
    for s in range(layers):
        enc_in[s].wait()

        def encode(j, carry, s=s):
            cols = pl.ds(pl.multiple_of(j * tile, tile), tile)
            part[s, :, cols] = jnp.dot(acts[s], encw[s, :, cols], preferred_element_type=F32)
            return carry

        lax.fori_loop(0, fdev // tile, encode, 0)
        moving[s] = scatter_send(part, rxf, s, 0)

    for t in range(layers):
        acc[t] = jnp.zeros((tokens, width), F32)

    def finish_forward(s, keep, total):
        feat[s, keep] = jnp.maximum(total + enc_bias[s], 0.0).astype(BF16)

    stage = {t: 0 for t in range(layers)}
    inflight = {}
    own = pl.ds(pl.multiple_of(core * half, half), half)
    theirs = pl.ds(pl.multiple_of((1 - core) * half, half), half)

    def advance(t):
        if stage[t] == 0:
            psend[t] = acc[t, theirs].astype(BF16)
            inflight[t] = [send(psend.at[t], prx.at[t], {"feat": partner})]
        elif stage[t] == 1:
            inflight[t][0].wait_recv()
            total = acc[t, own] + prx[t].astype(F32)
            acc[t, own] = total
            zsend[t] = total.reshape(groups, rows, width).astype(zsend.dtype)
            inflight[t] = [
                send(zsend.at[t, (zpos + d) % groups], zrx.at[t, d - 1], {"feat": zpeer[d]})
                for d in range(1, groups)
            ]
        elif stage[t] == 2:
            mine = pl.ds(pl.multiple_of(core * half + zpos * rows, rows), rows)
            total = acc[t, mine]
            for d in range(1, groups):
                inflight[t][d - 1].wait_recv()
                total = total + zrx[t, d - 1].astype(F32)
            total = total + dec_bias[t] - acts_out[t, core, zpos].astype(F32)
            errw[t, core, zpos] = total.astype(BF16).astype(errw.dtype)
            inflight[t] = [
                send(errw.at[t, core, zpos], errw.at[t, core, zpos], {"feat": zpeer[d]})
                for d in range(1, groups)
            ]
        elif stage[t] == 3:
            for c in inflight[t]:
                c.wait_recv()
            inflight[t] = [send(errw.at[t, core], errw.at[t, core], {"feat": partner})]
        elif stage[t] == 4:
            inflight[t][0].wait_recv()
            errb[t] = errw[t].reshape(tokens, width).astype(BF16)
            outs.append(local_copy(errb.at[t], err_out.at[t]))
        stage[t] += 1

    ktile = min(512, fdev)

    def decode(a, b):
        p = pair_list.index((a, b))
        dec_in[p].wait()

        def body(j, carry):
            cols = pl.ds(pl.multiple_of(j * ktile, ktile), ktile)
            acc[b] += jnp.dot(feat[a, :, cols], decw[p, cols, :], preferred_element_type=F32)
            return carry

        lax.fori_loop(0, fdev // ktile, body, 0)

    def arrived_forward(s):
        out = local_copy(feat.at[s], feat_out.at[s])
        for b in range(s, layers):
            decode(s, b)
            for t in range(s):
                if stage[t] < 5:
                    advance(t)
            if b == s:
                advance(s)
        return out

    exchange(part, rxf, feat, range(layers), moving, finish_forward, arrived_forward)
    for t in range(layers - 1):
        while stage[t] < 5:
            advance(t)
            if stage[layers - 1] < 2:
                advance(layers - 1)

    last = layers - 1

    def upstream_tile(a, b, cols):
        p = pair_list.index((a, b))
        return lax.dot_general(
            errb[b], decw[p, cols, :], (((1,), (1,)), ((), ())), preferred_element_type=F32
        )

    while stage[last] < 3:
        advance(last)
    drain()

    def early(a):
        def body(j, carry):
            cols = pl.ds(pl.multiple_of(j * tile, tile), tile)
            total = upstream_tile(a, a, cols)
            for b in range(a + 1, last):
                total = total + upstream_tile(a, b, cols)
            part[a, :, cols] = total
            return carry

        lax.fori_loop(0, fdev // tile, body, 0)

    for a in range(last):
        early(a)
        if stage[last] < 5:
            advance(last)
    while stage[last] < 5:
        advance(last)

    moving = {}
    backward = range(layers - 1, -1, -1)
    for a in backward:
        def late(j, carry, a=a):
            cols = pl.ds(pl.multiple_of(j * tile, tile), tile)
            total = upstream_tile(a, last, cols)
            if a < last:
                total = total + part[a, :, cols]
            ub[a, :, cols] = total.astype(BF16)
            return carry

        lax.fori_loop(0, fdev // tile, late, 0)
        moving[a] = scatter_send(ub, rxu, a, 0)

    square = jnp.zeros((1, width), F32)
    for t in range(layers):
        e = errb[t].astype(F32)
        square = square + jnp.sum(e * e, axis=0, keepdims=True)
    ms[0] = jnp.broadcast_to(square, (8, width))
    for i in range(bits):
        c = send(ms.at[i], mrx.at[i], {"slot": across[i]})
        c.wait_recv()
        ms[i + 1] = ms[i] + mrx[i]
    sq_out[...] = ms[bits]

    def finish_backward(s, keep, total):
        active = feat[s, keep].astype(F32) > 0.0
        delta[s, keep] = jnp.where(active, total, 0.0).astype(BF16)

    exchange(
        ub, rxu, delta, backward, moving, finish_backward,
        lambda s: local_copy(delta.at[s], delta_out.at[s]),
    )
    drain()
    for c in outs:
        c.wait()


def local(n_slot, n_feat, acts_in, acts_out, enc_weight, enc_bias, dec_weight, dec_bias):
    layers, tokens, width = acts_in.shape
    fdev = enc_weight.shape[2]
    n_pairs = dec_weight.shape[0]
    half, groups, bits = tokens // 2, n_feat // 2, bits_of(n_slot)
    rows = half // groups
    wire = BF16 if rows % 16 == 0 else F32
    landed = half - (half >> bits)
    remote = layers * bits * 2 * 2 * 2 + layers * 2 * groups + bits
    vmem = pl.BlockSpec(memory_space=pltpu.VMEM)
    hbm = pl.BlockSpec(memory_space=pl.ANY)
    features, error, delta, squares = pl.pallas_call(
        functools.partial(step_kernel, n_slot, n_feat),
        out_shape=(
            jax.ShapeDtypeStruct((layers, tokens, fdev), BF16),
            jax.ShapeDtypeStruct((layers, tokens, width), BF16),
            jax.ShapeDtypeStruct((layers, tokens, fdev), BF16),
            jax.ShapeDtypeStruct((8, width), F32),
        ),
        in_specs=[vmem, hbm, vmem, hbm, vmem, vmem],
        out_specs=(hbm, hbm, hbm, vmem),
        scratch_shapes=[
            pltpu.VMEM((layers, width, fdev), BF16),
            pltpu.VMEM((n_pairs, fdev, width), BF16),
            pltpu.VMEM((layers, tokens, fdev), F32),
            pltpu.VMEM((layers, 2, landed, fdev), F32),
            pltpu.VMEM((layers, tokens, fdev), BF16),
            pltpu.VMEM((layers, tokens, width), F32),
            pltpu.VMEM((layers, half, width), BF16),
            pltpu.VMEM((layers, half, width), BF16),
            pltpu.VMEM((layers, groups, rows, width), wire),
            pltpu.VMEM((layers, groups - 1, rows, width), wire),
            pltpu.VMEM((layers, 2, groups, rows, width), wire),
            pltpu.VMEM((layers, tokens, width), BF16),
            pltpu.VMEM((layers, tokens, fdev), BF16),
            pltpu.VMEM((layers, 2, landed, fdev), BF16),
            pltpu.VMEM((layers, tokens, fdev), BF16),
            pltpu.VMEM((bits + 1, 8, width), F32),
            pltpu.VMEM((bits, 8, width), F32),
            pltpu.SemaphoreType.DMA((4 * layers + n_pairs,)),
            pltpu.SemaphoreType.DMA((remote,)),
            pltpu.SemaphoreType.DMA((remote,)),
        ],
        compiler_params=pltpu.CompilerParams(
            collective_id=0, has_side_effects=True, vmem_limit_bytes=63 << 20
        ),
    )(
        acts_in, enc_weight, enc_bias.reshape(layers, 1, fdev), dec_weight,
        acts_out.reshape(layers, 2, groups, rows, width), dec_bias.reshape(layers, 1, width),
    )
    mse = jnp.sum(squares[0]) / (layers * tokens * width * n_slot)
    dec_grads = [
        lax.dot_general(
            features[a], error[b], (((0,), (0,)), ((), ())), preferred_element_type=F32
        )
        for a, b in pairs_of(layers)
    ]
    enc_grads = lax.dot_general(
        acts_in, delta, (((1,), (1,)), ((0,), (0,))), preferred_element_type=F32
    )
    bias_grad = jnp.sum(delta.astype(F32), axis=1)
    return enc_grads, bias_grad, jnp.stack(dec_grads), mse


def solution(mesh):
    in_specs = (
        P(None, None, "slot"),
        P(None, None, "slot"),
        P(None, "slot", "feat"),
        P(None, "feat"),
        P(None, "feat", "slot"),
        P(None, "slot"),
    )
    out_specs = (P(None, "slot", "feat"), P(None, "feat"), P(None, "feat", "slot"), P())
    body = functools.partial(local, mesh.shape["slot"], mesh.shape["feat"])
    return jax.shard_map(body, mesh=mesh, in_specs=in_specs, out_specs=out_specs, check_vma=False)
```

```python
import functools

import jax
import jax.numpy as jnp
from jax import lax
from jax.experimental import pallas as pl
from jax.experimental.pallas import tpu as pltpu
from jax.sharding import PartitionSpec as P

MESH = pl.DeviceIdType.MESH
F32, BF16 = jnp.float32, jnp.bfloat16


def pairs_of(layers):
    return [(a, b) for a in range(layers) for b in range(a, layers)]


def bits_of(n_slot):
    bits = n_slot.bit_length() - 1
    assert 1 << bits == n_slot
    return bits


def chunks_of(tokens, n_slot, n_feat):
    small = min(tokens // 4 >> bits_of(n_slot), tokens // 4 // (n_feat // 2))
    return 2 if small % 16 == 0 else 1


def step_kernel(
    n_slot, n_feat,
    acts, enc_hbm, enc_bias, dec_hbm, acts_out, dec_bias,
    feat_out, err_out, delta_out, mse_out,
    encw, decw, acts_t, target, part, rxf, feat, acc, psend, prx, zsend, zrx, errw, errb, errt,
    ub, rxu, delta, ms, mrx,
    local_sem, send_sem, recv_sem,
):
    layers, width, tokens = acts.shape
    fdev = encw.shape[2]
    chunks = chunks_of(tokens, n_slot, n_feat)
    span = tokens // chunks
    half = span // 2
    groups = n_feat // 2
    rows = half // groups
    bits = bits_of(n_slot)
    pair_list = pairs_of(layers)
    n_pairs = len(pair_list)
    slot = lax.axis_index("slot")
    fidx = lax.axis_index("feat")
    core = fidx % 2
    zpos = fidx // 2
    bit = [(slot // (1 << i)) % 2 for i in range(bits)]
    across = [slot + (1 - 2 * bit[i]) * (1 << i) for i in range(bits)]
    partner = fidx + 1 - 2 * core
    zpeer = [((zpos + d) % groups) * 2 + core for d in range(groups)]

    n_local = [0]
    outs = []

    def local_copy(src, dst):
        c = pltpu.make_async_copy(src, dst, local_sem.at[n_local[0]])
        n_local[0] += 1
        c.start()
        return c

    enc_in = [local_copy(enc_hbm.at[s], encw.at[s]) for s in range(layers)]
    dec_in = [local_copy(dec_hbm.at[p], decw.at[p]) for p in range(n_pairs)]

    barrier = pltpu.get_barrier_semaphore()
    for i in range(bits):
        pl.semaphore_signal(barrier, inc=1, device_id={"slot": across[i]}, device_id_type=MESH)
    for peer in [partner] + zpeer[1:]:
        pl.semaphore_signal(barrier, inc=1, device_id={"feat": peer}, device_id_type=MESH)
    for s in range(layers):
        acts_t[s] = acts[s].T
    pl.semaphore_wait(barrier, bits + groups)

    n_remote = [0]
    unsent = []

    def send(src, dst, device):
        c = pltpu.make_async_remote_copy(
            src_ref=src, dst_ref=dst,
            send_sem=send_sem.at[n_remote[0]], recv_sem=recv_sem.at[n_remote[0]],
            device_id=device, device_id_type=MESH,
        )
        n_remote[0] += 1
        c.start()
        unsent.append(c)
        return c

    orders = (list(range(bits)), list(range(bits))[::-1])

    def rows_of(c):
        return pl.ds(c * span, span)

    def start_row(c, h, phase):
        at = c * span + h * half
        for j in range(phase):
            at = at + bit[orders[h][j]] * (half >> (j + 1))
        return at

    def block(c, h, phase):
        size = half >> phase
        return pl.ds(pl.multiple_of(start_row(c, h, phase), size), size)

    def other(c, h, phase):
        size = half >> (phase + 1)
        at = start_row(c, h, phase) + (1 - bit[orders[h][phase]]) * size
        return pl.ds(pl.multiple_of(at, size), size)

    def land(phase):
        return pl.ds(half - (half >> phase), half >> (phase + 1))

    def scatter_send(buf, rx, c, s, phase):
        return [
            send(buf.at[s, other(c, h, phase)], rx.at[s, 2 * c + h, land(phase)],
                 {"slot": across[orders[h][phase]]})
            for h in range(2)
        ]

    def gather_send(full, c, s, phase):
        return [
            send(full.at[s, block(c, h, phase + 1)], full.at[s, block(c, h, phase + 1)],
                 {"slot": across[orders[h][phase]]})
            for h in range(2)
        ]

    moving = {}

    def scatter_step(buf, rx, full, finish, c, s, phase):
        for h in range(2):
            moving[c, s][h].wait_recv()
            keep = block(c, h, phase + 1)
            got = buf[s, keep].astype(F32) + rx[s, 2 * c + h, land(phase)].astype(F32)
            if phase + 1 < bits:
                buf[s, keep] = got.astype(buf.dtype)
            else:
                finish(s, keep, got)
        if phase + 1 < bits:
            moving[c, s] = scatter_send(buf, rx, c, s, phase + 1)
        else:
            moving[c, s] = gather_send(full, c, s, bits - 1)

    def gather_step(full, c, s, phase):
        for copy in moving[c, s]:
            copy.wait_recv()
        if phase >= 0:
            moving[c, s] = gather_send(full, c, s, phase)

    tile = min(256, fdev)
    ktile = min(512, fdev)

    def columns(j, size):
        return pl.ds(pl.multiple_of(j * size, size), size)

    def encode(c, s):
        if c == 0:
            enc_in[s].wait()

        def body(j, carry):
            cols = columns(j, tile)
            part[s, rows_of(c), cols] = jnp.dot(
                acts_t[s, rows_of(c), :], encw[s, :, cols], preferred_element_type=F32
            )
            return carry

        lax.fori_loop(0, fdev // tile, body, 0)

    def forward_send(c, s):
        moving[c, s] = scatter_send(part, rxf, c, s, 0)

    def finish_forward(s, keep, total):
        feat[s, keep] = jnp.maximum(total + enc_bias[s : s + 1, :], 0.0).astype(BF16)

    def prepare():
        for t in range(layers):
            acc[t] = jnp.zeros((tokens, width), F32)
            target[t] = dec_bias[t : t + 1, :] - acts_out[t].T.astype(F32)

    def decode(c, a):
        gather_step(feat, c, a, -1)
        outs.append(local_copy(feat.at[a, rows_of(c)], feat_out.at[a, rows_of(c)]))
        for b in range(a, layers):
            p = pair_list.index((a, b))
            if c == 0:
                dec_in[p].wait()

            def body(j, carry, b=b, p=p):
                cols = columns(j, ktile)
                acc[b, rows_of(c)] += lax.dot_general(
                    feat[a, rows_of(c), cols], decw[p, :, cols],
                    (((1,), (1,)), ((), ())), preferred_element_type=F32,
                )
                return carry

            lax.fori_loop(0, fdev // ktile, body, 0)

    summing = {}

    def reconstruct(c, stage):
        own = pl.ds(pl.multiple_of(c * span + core * half, half), half)
        theirs = pl.ds(pl.multiple_of(c * span + (1 - core) * half, half), half)
        mine = pl.ds(pl.multiple_of(c * span + core * half + zpos * rows, rows), rows)
        if stage == 0:
            for t in range(layers):
                psend[c, t] = acc[t, theirs].astype(BF16)
            summing[c] = [send(psend.at[c], prx.at[c], {"feat": partner})]
        elif stage == 1:
            summing[c][0].wait_recv()
            for t in range(layers):
                total = acc[t, own] + prx[c, t].astype(F32)
                acc[t, own] = total
                zsend[c, :, t] = total.reshape(groups, rows, width).astype(zsend.dtype)
            summing[c] = [
                send(zsend.at[c, (zpos + d) % groups], zrx.at[c, d - 1], {"feat": zpeer[d]})
                for d in range(1, groups)
            ]
        elif stage == 2:
            for copy in summing[c]:
                copy.wait_recv()
            for t in range(layers):
                total = acc[t, mine]
                for d in range(1, groups):
                    total = total + zrx[c, d - 1, t].astype(F32)
                total = total + target[t, mine]
                errw[c, core, zpos, t] = total.astype(BF16).astype(errw.dtype)
            summing[c] = [
                send(errw.at[c, core, zpos], errw.at[c, core, zpos], {"feat": zpeer[d]})
                for d in range(1, groups)
            ]
        elif stage == 3:
            for copy in summing[c]:
                copy.wait_recv()
            summing[c] = [send(errw.at[c, core], errw.at[c, core], {"feat": partner})]
        elif stage == 4:
            summing[c][0].wait_recv()
            for t in range(layers):
                errb[t, rows_of(c)] = errw[c, :, :, t].reshape(span, width).astype(BF16)

    def upstream(c, a):
        def body(j, carry):
            cols = columns(j, tile)
            total = None
            for b in range(a, layers):
                term = jnp.dot(
                    errb[b, rows_of(c), :], decw[pair_list.index((a, b)), :, cols],
                    preferred_element_type=F32,
                )
                total = term if total is None else total + term
            ub[a, rows_of(c), cols] = total.astype(BF16)
            return carry

        lax.fori_loop(0, fdev // tile, body, 0)
        moving[c, a] = scatter_send(ub, rxu, c, a, 0)

    def finish_backward(s, keep, total):
        active = feat[s, keep].astype(F32) > 0.0
        delta[s, keep] = jnp.where(active, total, 0.0).astype(BF16)

    def arrive(c, s):
        gather_step(delta, c, s, -1)
        outs.append(local_copy(delta.at[s, rows_of(c)], delta_out.at[s, rows_of(c)]))

    def errors_out():
        square = jnp.zeros((1, width), F32)
        for t in range(layers):
            e = errb[t].astype(F32)
            square = square + jnp.sum(e * e, axis=0, keepdims=True)
            errt[t] = errb[t].T
        outs.append(local_copy(errt, err_out))
        ms[0] = jnp.broadcast_to(square, (8, width))
        summing["m"] = send(ms.at[0], mrx.at[0], {"slot": across[0]})

    def errors_sum(i):
        summing["m"].wait_recv()
        ms[i + 1] = ms[i] + mrx[i]
        if i + 1 < bits:
            summing["m"] = send(ms.at[i + 1], mrx.at[i + 1], {"slot": across[i + 1]})
        else:
            count = layers * tokens * width * n_slot
            mse_out[...] = jnp.sum(ms[bits, 0:1, :], axis=1, keepdims=True) / count

    up, down = range(layers), range(layers - 1, -1, -1)

    def forward_scatter(c, phase, order=up):
        for s in order:
            scatter_step(part, rxf, feat, finish_forward, c, s, phase)

    def forward_gather(c):
        for phase in range(bits - 2, -1, -1):
            for s in up:
                gather_step(feat, c, s, phase)

    def backward_scatter(c, phase):
        for s in down:
            scatter_step(ub, rxu, delta, finish_backward, c, s, phase)

    def backward_gather(c):
        for phase in range(bits - 2, -1, -1):
            for s in down:
                gather_step(delta, c, s, phase)

    for s in up:
        encode(0, s)
        forward_send(0, s)
    prepare()
    if chunks == 2:
        for s in up:
            encode(1, s)
    for phase in range(bits):
        forward_scatter(0, phase)
    if chunks == 1:
        forward_gather(0)
        for s in up:
            decode(0, s)
        for stage in range(5):
            reconstruct(0, stage)
        for s in down:
            upstream(0, s)
        errors_out()
        for phase in range(bits):
            backward_scatter(0, phase)
            errors_sum(phase)
        backward_gather(0)
        for s in down:
            arrive(0, s)
    else:
        forward_send(1, 0)
        forward_gather(0)
        for s in up[1:]:
            forward_send(1, s)
        for s in up:
            decode(0, s)
        reconstruct(0, 0)
        for phase in range(bits - 1):
            forward_scatter(1, phase)
            if phase == 0:
                reconstruct(0, 1)
                reconstruct(0, 2)
        reconstruct(0, 3)
        forward_scatter(1, bits - 1)
        reconstruct(0, 4)
        upstream(0, layers - 1)
        forward_gather(1)
        for s in down[1:]:
            upstream(0, s)
        for s in up:
            decode(1, s)
        reconstruct(1, 0)
        backward_scatter(0, 0)
        reconstruct(1, 1)
        for phase in range(1, bits):
            backward_scatter(0, phase)
        reconstruct(1, 2)
        backward_gather(0)
        reconstruct(1, 3)
        reconstruct(1, 4)
        for s in down:
            upstream(1, s)
        errors_out()
        for s in down:
            arrive(0, s)
        for phase in range(bits):
            backward_scatter(1, phase)
            errors_sum(phase)
        backward_gather(1)
        for s in down:
            arrive(1, s)
    for c in unsent:
        c.wait_send()
    for c in outs:
        c.wait()


def gradient_kernel(n_pairs, err, feat, acts, delta, dec_grad, enc_grad, bias_grad):
    item, j = pl.program_id(0), pl.program_id(1)

    @pl.when(item < n_pairs)
    def _():
        dec_grad[0] = jnp.dot(err[0], feat[0], preferred_element_type=F32)

    @pl.when(item >= n_pairs)
    def _():
        enc_grad[0] = jnp.dot(acts[0], delta[0], preferred_element_type=F32)
        size = delta.shape[2]
        cols = pl.ds(pl.multiple_of(j * size, size), size)
        total = jnp.sum(delta[0].astype(F32), axis=0, keepdims=True)
        bias_grad[pl.ds(item - n_pairs, 1), cols] = total


def gradients(err, feat, acts, delta):
    layers, width, tokens = err.shape
    fdev = feat.shape[2]
    n_pairs = len(pairs_of(layers))
    tile = min(1024, fdev)
    tiles = fdev // tile
    firsts = [pairs_of(layers).index((a, a)) for a in range(layers)]

    def source(p):
        a = 0
        for first in firsts[1:]:
            a = a + jnp.where(p >= first, 1, 0)
        return a

    def dest(p):
        b = p
        for k, first in enumerate(firsts):
            if k:
                b = b - jnp.where(p >= first, first - firsts[k - 1] - 1, 0)
        return b

    def pair(i):
        return jnp.minimum(i, n_pairs - 1)

    def layer(i):
        return jnp.maximum(i - n_pairs, 0)

    def early(i, j):
        return jnp.where(i < n_pairs, j, tiles - 1)

    def late(i, j):
        return jnp.where(i < n_pairs, 0, j)

    return pl.pallas_call(
        functools.partial(gradient_kernel, n_pairs),
        grid=(n_pairs + layers, tiles),
        out_shape=(
            jax.ShapeDtypeStruct((n_pairs, width, fdev), F32),
            jax.ShapeDtypeStruct((layers, width, fdev), F32),
            jax.ShapeDtypeStruct((layers, fdev), F32),
        ),
        in_specs=[
            pl.BlockSpec((1, width, tokens), lambda i, j: (dest(pair(i)), 0, 0)),
            pl.BlockSpec((1, tokens, tile), lambda i, j: (source(pair(i)), 0, early(i, j))),
            pl.BlockSpec((1, width, tokens), lambda i, j: (layer(i), 0, 0)),
            pl.BlockSpec((1, tokens, tile), lambda i, j: (layer(i), 0, late(i, j))),
        ],
        out_specs=(
            pl.BlockSpec((1, width, tile), lambda i, j: (pair(i), 0, early(i, j))),
            pl.BlockSpec((1, width, tile), lambda i, j: (layer(i), 0, late(i, j))),
            pl.BlockSpec((layers, fdev), lambda i, j: (0, 0)),
        ),
        compiler_params=pltpu.CompilerParams(dimension_semantics=("arbitrary", "arbitrary")),
    )(err, feat, acts, delta)


def local(n_slot, n_feat, acts_in, acts_out, enc_weight, enc_bias, dec_weight, dec_bias):
    layers, tokens, width = acts_in.shape
    fdev = enc_weight.shape[2]
    n_pairs = dec_weight.shape[0]
    chunks = chunks_of(tokens, n_slot, n_feat)
    half, groups, bits = tokens // chunks // 2, n_feat // 2, bits_of(n_slot)
    rows = half // groups
    wire = BF16 if rows % 16 == 0 else F32
    landed = half - (half >> bits)
    remote = chunks * (layers * bits * 2 * 2 * 2 + 2 * groups) + bits
    vmem = pl.BlockSpec(memory_space=pltpu.VMEM)
    hbm = pl.BlockSpec(memory_space=pl.ANY)
    acts = jnp.transpose(acts_in, (0, 2, 1))
    features, error, delta, mse = pl.pallas_call(
        functools.partial(step_kernel, n_slot, n_feat),
        out_shape=(
            jax.ShapeDtypeStruct((layers, tokens, fdev), BF16),
            jax.ShapeDtypeStruct((layers, width, tokens), BF16),
            jax.ShapeDtypeStruct((layers, tokens, fdev), BF16),
            jax.ShapeDtypeStruct((1, 1), F32),
        ),
        in_specs=[vmem, hbm, vmem, hbm, vmem, vmem],
        out_specs=(hbm, hbm, hbm, vmem),
        scratch_shapes=[
            pltpu.VMEM((layers, width, fdev), BF16),
            pltpu.VMEM((n_pairs, width, fdev), BF16),
            pltpu.VMEM((layers, tokens, width), BF16),
            pltpu.VMEM((layers, tokens, width), F32),
            pltpu.VMEM((layers, tokens, fdev), F32),
            pltpu.VMEM((layers, 2 * chunks, landed, fdev), F32),
            pltpu.VMEM((layers, tokens, fdev), BF16),
            pltpu.VMEM((layers, tokens, width), F32),
            pltpu.VMEM((chunks, layers, half, width), BF16),
            pltpu.VMEM((chunks, layers, half, width), BF16),
            pltpu.VMEM((chunks, groups, layers, rows, width), wire),
            pltpu.VMEM((chunks, groups - 1, layers, rows, width), wire),
            pltpu.VMEM((chunks, 2, groups, layers, rows, width), wire),
            pltpu.VMEM((layers, tokens, width), BF16),
            pltpu.VMEM((layers, width, tokens), BF16),
            pltpu.VMEM((layers, tokens, fdev), BF16),
            pltpu.VMEM((layers, 2 * chunks, landed, fdev), BF16),
            pltpu.VMEM((layers, tokens, fdev), BF16),
            pltpu.VMEM((bits + 1, 8, width), F32),
            pltpu.VMEM((bits, 8, width), F32),
            pltpu.SemaphoreType.DMA((layers + n_pairs + 2 * chunks * layers + 1,)),
            pltpu.SemaphoreType.DMA((remote,)),
            pltpu.SemaphoreType.DMA((remote,)),
        ],
        compiler_params=pltpu.CompilerParams(
            collective_id=0, has_side_effects=True, vmem_limit_bytes=63 << 20
        ),
    )(
        acts, enc_weight, enc_bias, jnp.transpose(dec_weight, (0, 2, 1)),
        jnp.transpose(acts_out, (0, 2, 1)), dec_bias,
    )
    dec_grads, enc_grads, bias_grads = gradients(error, features, acts, delta)
    return enc_grads, bias_grads, jnp.transpose(dec_grads, (0, 2, 1)), mse.reshape(())


def solution(mesh):
    in_specs = (
        P(None, None, "slot"),
        P(None, None, "slot"),
        P(None, "slot", "feat"),
        P(None, "feat"),
        P(None, "feat", "slot"),
        P(None, "slot"),
    )
    out_specs = (P(None, "slot", "feat"), P(None, "feat"), P(None, "feat", "slot"), P())
    body = functools.partial(local, mesh.shape["slot"], mesh.shape["feat"])
    return jax.shard_map(body, mesh=mesh, in_specs=in_specs, out_specs=out_specs, check_vma=False)
```

```python
import functools

import jax
import jax.numpy as jnp
from jax import lax
from jax.experimental import pallas as pl
from jax.experimental.pallas import tpu as pltpu
from jax.sharding import PartitionSpec as P

MESH = pl.DeviceIdType.MESH
F32, BF16 = jnp.float32, jnp.bfloat16


def pairs_of(layers):
    return [(a, b) for a in range(layers) for b in range(a, layers)]


def bits_of(n_slot):
    bits = n_slot.bit_length() - 1
    assert 1 << bits == n_slot
    return bits


def chunks_of(tokens, n_slot, n_feat):
    small = min(tokens // 4 >> bits_of(n_slot), tokens // 4 // (n_feat // 2))
    return 2 if small % 16 == 0 else 1


def step_kernel(
    n_slot, n_feat,
    acts, enc_hbm, enc_bias, dec_hbm, acts_out, dec_bias,
    feat_out, err_out, delta_out, mse_out,
    encw, decw, acts_t, target, part, rxf, feat, acc, psend, prx, zsend, zrx, errw, errb, errt,
    ub, rxu, delta, ms, mrx,
    local_sem, send_sem, recv_sem,
):
    layers, width, tokens = acts.shape
    fdev = encw.shape[2]
    chunks = chunks_of(tokens, n_slot, n_feat)
    span = tokens // chunks
    half = span // 2
    groups = n_feat // 2
    rows = half // groups
    bits = bits_of(n_slot)
    pair_list = pairs_of(layers)
    n_pairs = len(pair_list)
    slot = lax.axis_index("slot")
    fidx = lax.axis_index("feat")
    core = fidx % 2
    zpos = fidx // 2
    bit = [(slot // (1 << i)) % 2 for i in range(bits)]
    across = [slot + (1 - 2 * bit[i]) * (1 << i) for i in range(bits)]
    partner = fidx + 1 - 2 * core
    zpeer = [((zpos + d) % groups) * 2 + core for d in range(groups)]

    n_local = [0]
    outs = []

    def local_copy(src, dst):
        c = pltpu.make_async_copy(src, dst, local_sem.at[n_local[0]])
        n_local[0] += 1
        c.start()
        return c

    enc_in = [local_copy(enc_hbm.at[s], encw.at[s]) for s in range(layers)]
    dec_in = [local_copy(dec_hbm.at[p], decw.at[p]) for p in range(n_pairs)]

    barrier = pltpu.get_barrier_semaphore()
    for i in range(bits):
        pl.semaphore_signal(barrier, inc=1, device_id={"slot": across[i]}, device_id_type=MESH)
    for peer in [partner] + zpeer[1:]:
        pl.semaphore_signal(barrier, inc=1, device_id={"feat": peer}, device_id_type=MESH)
    for s in range(layers):
        acts_t[s] = acts[s].T
    pl.semaphore_wait(barrier, bits + groups)

    n_remote = [0]
    unsent = []

    def send(src, dst, device):
        c = pltpu.make_async_remote_copy(
            src_ref=src, dst_ref=dst,
            send_sem=send_sem.at[n_remote[0]], recv_sem=recv_sem.at[n_remote[0]],
            device_id=device, device_id_type=MESH,
        )
        n_remote[0] += 1
        c.start()
        unsent.append(c)
        return c

    orders = (list(range(bits)), list(range(bits))[::-1])

    def rows_of(c):
        return pl.ds(c * span, span)

    def start_row(c, h, phase):
        at = c * span + h * half
        for j in range(phase):
            at = at + bit[orders[h][j]] * (half >> (j + 1))
        return at

    def block(c, h, phase):
        size = half >> phase
        return pl.ds(pl.multiple_of(start_row(c, h, phase), size), size)

    def other(c, h, phase):
        size = half >> (phase + 1)
        at = start_row(c, h, phase) + (1 - bit[orders[h][phase]]) * size
        return pl.ds(pl.multiple_of(at, size), size)

    def land(phase):
        return pl.ds(half - (half >> phase), half >> (phase + 1))

    def scatter_send(buf, rx, c, s, phase):
        return [
            send(buf.at[s, other(c, h, phase)], rx.at[s, 2 * c + h, land(phase)],
                 {"slot": across[orders[h][phase]]})
            for h in range(2)
        ]

    def gather_send(full, c, s, phase):
        return [
            send(full.at[s, block(c, h, phase + 1)], full.at[s, block(c, h, phase + 1)],
                 {"slot": across[orders[h][phase]]})
            for h in range(2)
        ]

    moving = {}

    def scatter_step(buf, rx, full, finish, c, s, phase):
        for h in range(2):
            moving[c, s][h].wait_recv()
            keep = block(c, h, phase + 1)
            got = buf[s, keep].astype(F32) + rx[s, 2 * c + h, land(phase)].astype(F32)
            if phase + 1 < bits:
                buf[s, keep] = got.astype(buf.dtype)
            else:
                finish(s, keep, got)
        if phase + 1 < bits:
            moving[c, s] = scatter_send(buf, rx, c, s, phase + 1)
        else:
            moving[c, s] = gather_send(full, c, s, bits - 1)

    def gather_step(full, c, s, phase):
        for copy in moving[c, s]:
            copy.wait_recv()
        if phase >= 0:
            moving[c, s] = gather_send(full, c, s, phase)

    tile = min(256, fdev)
    ktile = min(512, fdev)

    def columns(j, size):
        return pl.ds(pl.multiple_of(j * size, size), size)

    def encode(c, s):
        if c == 0:
            enc_in[s].wait()

        def body(j, carry):
            cols = columns(j, tile)
            part[s, rows_of(c), cols] = jnp.dot(
                acts_t[s, rows_of(c), :], encw[s, :, cols], preferred_element_type=F32
            )
            return carry

        lax.fori_loop(0, fdev // tile, body, 0)

    def forward_send(c, s):
        moving[c, s] = scatter_send(part, rxf, c, s, 0)

    def finish_forward(s, keep, total):
        feat[s, keep] = jnp.maximum(total + enc_bias[s : s + 1, :], 0.0).astype(BF16)

    def prepare():
        for t in range(layers):
            acc[t] = jnp.zeros((tokens, width), F32)
            target[t] = dec_bias[t : t + 1, :] - acts_out[t].T.astype(F32)

    def decode(c, a):
        gather_step(feat, c, a, -1)
        outs.append(local_copy(feat.at[a, rows_of(c)], feat_out.at[a, rows_of(c)]))
        for b in range(a, layers):
            p = pair_list.index((a, b))
            if c == 0:
                dec_in[p].wait()

            def body(j, carry, b=b, p=p):
                cols = columns(j, ktile)
                acc[b, rows_of(c)] += lax.dot_general(
                    feat[a, rows_of(c), cols], decw[p, :, cols],
                    (((1,), (1,)), ((), ())), preferred_element_type=F32,
                )
                return carry

            lax.fori_loop(0, fdev // ktile, body, 0)

    summing = {}

    def reconstruct(c, stage):
        own = pl.ds(pl.multiple_of(c * span + core * half, half), half)
        theirs = pl.ds(pl.multiple_of(c * span + (1 - core) * half, half), half)
        mine = pl.ds(pl.multiple_of(c * span + core * half + zpos * rows, rows), rows)
        if stage == 0:
            for t in range(layers):
                psend[c, t] = acc[t, theirs].astype(BF16)
            summing[c] = [send(psend.at[c], prx.at[c], {"feat": partner})]
        elif stage == 1:
            summing[c][0].wait_recv()
            for t in range(layers):
                total = acc[t, own] + prx[c, t].astype(F32)
                acc[t, own] = total
                zsend[c, :, t] = total.reshape(groups, rows, width).astype(zsend.dtype)
            summing[c] = [
                send(zsend.at[c, (zpos + d) % groups], zrx.at[c, d - 1], {"feat": zpeer[d]})
                for d in range(1, groups)
            ]
        elif stage == 2:
            for copy in summing[c]:
                copy.wait_recv()
            for t in range(layers):
                total = acc[t, mine]
                for d in range(1, groups):
                    total = total + zrx[c, d - 1, t].astype(F32)
                total = total + target[t, mine]
                errw[c, core, zpos, t] = total.astype(BF16).astype(errw.dtype)
            summing[c] = [
                send(errw.at[c, core, zpos], errw.at[c, core, zpos], {"feat": zpeer[d]})
                for d in range(1, groups)
            ]
        elif stage == 3:
            for copy in summing[c]:
                copy.wait_recv()
            summing[c] = [send(errw.at[c, core], errw.at[c, core], {"feat": partner})]
        elif stage == 4:
            summing[c][0].wait_recv()
            for t in range(layers):
                errb[t, rows_of(c)] = errw[c, :, :, t].reshape(span, width).astype(BF16)

    def upstream(c, a):
        def body(j, carry):
            cols = columns(j, tile)
            total = None
            for b in range(a, layers):
                term = jnp.dot(
                    errb[b, rows_of(c), :], decw[pair_list.index((a, b)), :, cols],
                    preferred_element_type=F32,
                )
                total = term if total is None else total + term
            ub[a, rows_of(c), cols] = total.astype(BF16)
            return carry

        lax.fori_loop(0, fdev // tile, body, 0)
        moving[c, a] = scatter_send(ub, rxu, c, a, 0)

    def finish_backward(s, keep, total):
        active = feat[s, keep].astype(F32) > 0.0
        delta[s, keep] = jnp.where(active, total, 0.0).astype(BF16)

    def arrive(c, s):
        gather_step(delta, c, s, -1)
        outs.append(local_copy(delta.at[s, rows_of(c)], delta_out.at[s, rows_of(c)]))

    def errors_out():
        square = jnp.zeros((1, width), F32)
        for t in range(layers):
            e = errb[t].astype(F32)
            square = square + jnp.sum(e * e, axis=0, keepdims=True)
            errt[t] = errb[t].T
        outs.append(local_copy(errt, err_out))
        ms[0] = jnp.broadcast_to(square, (8, width))
        summing["m"] = send(ms.at[0], mrx.at[0], {"slot": across[0]})

    def errors_sum(i):
        summing["m"].wait_recv()
        ms[i + 1] = ms[i] + mrx[i]
        if i + 1 < bits:
            summing["m"] = send(ms.at[i + 1], mrx.at[i + 1], {"slot": across[i + 1]})
        else:
            count = layers * tokens * width * n_slot
            mse_out[...] = jnp.sum(ms[bits, 0:1, :], axis=1, keepdims=True) / count

    up, down = range(layers), range(layers - 1, -1, -1)

    def forward_scatter(c, phase, order=up):
        for s in order:
            scatter_step(part, rxf, feat, finish_forward, c, s, phase)

    def forward_gather(c):
        for phase in range(bits - 2, -1, -1):
            for s in up:
                gather_step(feat, c, s, phase)

    def backward_scatter(c, phase):
        for s in down:
            scatter_step(ub, rxu, delta, finish_backward, c, s, phase)

    def backward_gather(c):
        for phase in range(bits - 2, -1, -1):
            for s in down:
                gather_step(delta, c, s, phase)

    for s in up:
        encode(0, s)
        forward_send(0, s)
    prepare()
    if chunks == 2:
        for s in up:
            encode(1, s)
    for phase in range(bits):
        forward_scatter(0, phase)
    if chunks == 1:
        forward_gather(0)
        for s in up:
            decode(0, s)
        for stage in range(5):
            reconstruct(0, stage)
        for s in down:
            upstream(0, s)
        errors_out()
        for phase in range(bits):
            backward_scatter(0, phase)
            errors_sum(phase)
        backward_gather(0)
        for s in down:
            arrive(0, s)
    else:
        forward_send(1, 0)
        forward_gather(0)
        for s in up[1:]:
            forward_send(1, s)
        for s in up:
            decode(0, s)
        reconstruct(0, 0)
        work = [lambda k=k: reconstruct(0, k) for k in range(1, 5)]
        work.append(lambda: upstream(0, layers - 1))
        for phase in range(bits):
            for s in up:
                scatter_step(part, rxf, feat, finish_forward, 1, s, phase)
                if work and s % 3 != 2:
                    work.pop(0)()
        while work:
            work.pop(0)()
        forward_gather(1)
        for s in down[1:]:
            upstream(0, s)
        for s in up:
            decode(1, s)
        reconstruct(1, 0)
        backward_scatter(0, 0)
        reconstruct(1, 1)
        for phase in range(1, bits):
            backward_scatter(0, phase)
        reconstruct(1, 2)
        backward_gather(0)
        reconstruct(1, 3)
        reconstruct(1, 4)
        for s in down:
            upstream(1, s)
        errors_out()
        for s in down:
            arrive(0, s)
        for phase in range(bits):
            backward_scatter(1, phase)
            errors_sum(phase)
        backward_gather(1)
        for s in down:
            arrive(1, s)
    for c in unsent:
        c.wait_send()
    for c in outs:
        c.wait()


def gradient_kernel(
    err_hbm, feat_hbm, acts_hbm, delta_hbm, dec_grad, enc_grad, bias_grad,
    err, feat, acts, delta, ring, in_sem, out_sem,
):
    layers, width, _ = err.shape
    fdev = feat.shape[2]
    depth, _, tile = ring.shape
    parts = out_sem.shape[1]
    loads = {}
    n_loads = 0
    for s in range(layers):
        for name, src, dst in (("err", err_hbm, err), ("feat", feat_hbm, feat)):
            loads[name, s] = pltpu.make_async_copy(src.at[s], dst.at[s], in_sem.at[n_loads])
            loads[name, s].start()
            n_loads += 1
    for s in range(layers):
        for name, src, dst in (("acts", acts_hbm, acts), ("delta", delta_hbm, delta)):
            loads[name, s] = pltpu.make_async_copy(src.at[s], dst.at[s], in_sem.at[n_loads])
            loads[name, s].start()
            n_loads += 1

    def need(name, s):
        if (name, s) in loads:
            loads.pop((name, s)).wait()

    writing = []

    def product(left, right, out):
        for j in range(fdev // tile):
            n = len(writing)
            place = n % depth
            if n >= depth:
                for c in writing[n - depth]:
                    c.wait()
            cols = pl.ds(j * tile, tile)
            ring[place] = jnp.dot(left[...], right[:, cols], preferred_element_type=F32)
            size = width // parts
            copies = []
            for k in range(parts):
                some = pl.ds(k * size, size)
                copies.append(pltpu.make_async_copy(
                    ring.at[place, some], out.at[some, cols], out_sem.at[place, k]
                ))
                copies[-1].start()
            writing.append(copies)

    for p, (a, b) in enumerate(pairs_of(layers)):
        need("feat", a)
        need("err", b)
        product(err.at[b], feat.at[a], dec_grad.at[p])
    for s in range(layers):
        need("acts", s)
        need("delta", s)
        product(acts.at[s], delta.at[s], enc_grad.at[s])
        bias_grad[s : s + 1, :] = jnp.sum(delta[s].astype(F32), axis=0, keepdims=True)
    for copies in writing[-depth:]:
        for c in copies:
            c.wait()


def gradients(err, feat, acts, delta):
    layers, width, tokens = err.shape
    fdev = feat.shape[2]
    n_pairs = len(pairs_of(layers))
    tile = min(512, fdev)
    depth, parts = 8, 2
    hbm = pl.BlockSpec(memory_space=pl.ANY)
    return pl.pallas_call(
        gradient_kernel,
        out_shape=(
            jax.ShapeDtypeStruct((n_pairs, width, fdev), F32),
            jax.ShapeDtypeStruct((layers, width, fdev), F32),
            jax.ShapeDtypeStruct((layers, fdev), F32),
        ),
        in_specs=[hbm] * 4,
        out_specs=(hbm, hbm, pl.BlockSpec(memory_space=pltpu.VMEM)),
        scratch_shapes=[
            pltpu.VMEM((layers, width, tokens), BF16),
            pltpu.VMEM((layers, tokens, fdev), BF16),
            pltpu.VMEM((layers, width, tokens), BF16),
            pltpu.VMEM((layers, tokens, fdev), BF16),
            pltpu.VMEM((depth, width, tile), F32),
            pltpu.SemaphoreType.DMA((4 * layers,)),
            pltpu.SemaphoreType.DMA((depth, parts)),
        ],
        compiler_params=pltpu.CompilerParams(vmem_limit_bytes=60 << 20),
    )(err, feat, acts, delta)


def local(n_slot, n_feat, acts_in, acts_out, enc_weight, enc_bias, dec_weight, dec_bias):
    layers, tokens, width = acts_in.shape
    fdev = enc_weight.shape[2]
    n_pairs = dec_weight.shape[0]
    chunks = chunks_of(tokens, n_slot, n_feat)
    half, groups, bits = tokens // chunks // 2, n_feat // 2, bits_of(n_slot)
    rows = half // groups
    wire = BF16 if rows % 16 == 0 else F32
    landed = half - (half >> bits)
    remote = chunks * (layers * bits * 2 * 2 * 2 + 2 * groups) + bits
    vmem = pl.BlockSpec(memory_space=pltpu.VMEM)
    hbm = pl.BlockSpec(memory_space=pl.ANY)
    acts = jnp.transpose(acts_in, (0, 2, 1))
    features, error, delta, mse = pl.pallas_call(
        functools.partial(step_kernel, n_slot, n_feat),
        out_shape=(
            jax.ShapeDtypeStruct((layers, tokens, fdev), BF16),
            jax.ShapeDtypeStruct((layers, width, tokens), BF16),
            jax.ShapeDtypeStruct((layers, tokens, fdev), BF16),
            jax.ShapeDtypeStruct((1, 1), F32),
        ),
        in_specs=[vmem, hbm, vmem, hbm, vmem, vmem],
        out_specs=(hbm, hbm, hbm, vmem),
        scratch_shapes=[
            pltpu.VMEM((layers, width, fdev), BF16),
            pltpu.VMEM((n_pairs, width, fdev), BF16),
            pltpu.VMEM((layers, tokens, width), BF16),
            pltpu.VMEM((layers, tokens, width), F32),
            pltpu.VMEM((layers, tokens, fdev), F32),
            pltpu.VMEM((layers, 2 * chunks, landed, fdev), F32),
            pltpu.VMEM((layers, tokens, fdev), BF16),
            pltpu.VMEM((layers, tokens, width), F32),
            pltpu.VMEM((chunks, layers, half, width), BF16),
            pltpu.VMEM((chunks, layers, half, width), BF16),
            pltpu.VMEM((chunks, groups, layers, rows, width), wire),
            pltpu.VMEM((chunks, groups - 1, layers, rows, width), wire),
            pltpu.VMEM((chunks, 2, groups, layers, rows, width), wire),
            pltpu.VMEM((layers, tokens, width), BF16),
            pltpu.VMEM((layers, width, tokens), BF16),
            pltpu.VMEM((layers, tokens, fdev), BF16),
            pltpu.VMEM((layers, 2 * chunks, landed, fdev), BF16),
            pltpu.VMEM((layers, tokens, fdev), BF16),
            pltpu.VMEM((bits + 1, 8, width), F32),
            pltpu.VMEM((bits, 8, width), F32),
            pltpu.SemaphoreType.DMA((layers + n_pairs + 2 * chunks * layers + 1,)),
            pltpu.SemaphoreType.DMA((remote,)),
            pltpu.SemaphoreType.DMA((remote,)),
        ],
        compiler_params=pltpu.CompilerParams(
            collective_id=0, has_side_effects=True, vmem_limit_bytes=63 << 20
        ),
    )(
        acts, enc_weight, enc_bias, jnp.transpose(dec_weight, (0, 2, 1)),
        jnp.transpose(acts_out, (0, 2, 1)), dec_bias,
    )
    dec_grads, enc_grads, bias_grads = gradients(error, features, acts, delta)
    return enc_grads, bias_grads, jnp.transpose(dec_grads, (0, 2, 1)), mse.reshape(())


def solution(mesh):
    in_specs = (
        P(None, None, "slot"),
        P(None, None, "slot"),
        P(None, "slot", "feat"),
        P(None, "feat"),
        P(None, "feat", "slot"),
        P(None, "slot"),
    )
    out_specs = (P(None, "slot", "feat"), P(None, "feat"), P(None, "feat", "slot"), P())
    body = functools.partial(local, mesh.shape["slot"], mesh.shape["feat"])
    return jax.shard_map(body, mesh=mesh, in_specs=in_specs, out_specs=out_specs, check_vma=False)
```

```python
import functools

import jax
import jax.numpy as jnp
from jax import lax
from jax.experimental import pallas as pl
from jax.experimental.pallas import tpu as pltpu
from jax.sharding import PartitionSpec as P

MESH = pl.DeviceIdType.MESH
F32, BF16 = jnp.float32, jnp.bfloat16


def pairs_of(layers):
    return [(a, b) for a in range(layers) for b in range(a, layers)]


def bits_of(n_slot):
    bits = n_slot.bit_length() - 1
    assert 1 << bits == n_slot
    return bits


def chunks_of(tokens, n_slot, n_feat):
    small = min(tokens // 4 >> bits_of(n_slot), tokens // 4 // (n_feat // 2))
    return 2 if small % 16 == 0 else 1


def step_kernel(
    n_slot, n_feat,
    acts, enc_hbm, enc_bias, dec_hbm, acts_out, dec_bias,
    feat_out, err_out, delta_out, mse_out,
    encw, decw, acts_t, target, part, rxf, feat, acc, psend, prx, zsend, zrx, errw, errb, errt,
    ub, rxu, delta, ms, mrx,
    local_sem, send_sem, recv_sem,
):
    layers, width, tokens = acts.shape
    fdev = encw.shape[2]
    chunks = chunks_of(tokens, n_slot, n_feat)
    span = tokens // chunks
    half = span // 2
    groups = n_feat // 2
    rows = half // groups
    bits = bits_of(n_slot)
    pair_list = pairs_of(layers)
    n_pairs = len(pair_list)
    slot = lax.axis_index("slot")
    fidx = lax.axis_index("feat")
    core = fidx % 2
    zpos = fidx // 2
    bit = [(slot // (1 << i)) % 2 for i in range(bits)]
    across = [slot + (1 - 2 * bit[i]) * (1 << i) for i in range(bits)]
    partner = fidx + 1 - 2 * core
    zpeer = [((zpos + d) % groups) * 2 + core for d in range(groups)]

    n_local = [0]
    outs = []

    def local_copy(src, dst):
        c = pltpu.make_async_copy(src, dst, local_sem.at[n_local[0]])
        n_local[0] += 1
        c.start()
        return c

    enc_in = [local_copy(enc_hbm.at[s], encw.at[s]) for s in range(layers)]
    dec_in = [local_copy(dec_hbm.at[p], decw.at[p]) for p in range(n_pairs)]

    barrier = pltpu.get_barrier_semaphore()
    for i in range(bits):
        pl.semaphore_signal(barrier, inc=1, device_id={"slot": across[i]}, device_id_type=MESH)
    for peer in [partner] + zpeer[1:]:
        pl.semaphore_signal(barrier, inc=1, device_id={"feat": peer}, device_id_type=MESH)
    for s in range(layers):
        acts_t[s] = acts[s].T
    pl.semaphore_wait(barrier, bits + groups)

    n_remote = [0]
    unsent = []

    def send(src, dst, device):
        c = pltpu.make_async_remote_copy(
            src_ref=src, dst_ref=dst,
            send_sem=send_sem.at[n_remote[0]], recv_sem=recv_sem.at[n_remote[0]],
            device_id=device, device_id_type=MESH,
        )
        n_remote[0] += 1
        c.start()
        unsent.append(c)
        return c

    orders = (list(range(bits)), list(range(bits))[::-1])

    def rows_of(c):
        return pl.ds(c * span, span)

    def start_row(c, h, phase):
        at = c * span + h * half
        for j in range(phase):
            at = at + bit[orders[h][j]] * (half >> (j + 1))
        return at

    def block(c, h, phase):
        size = half >> phase
        return pl.ds(pl.multiple_of(start_row(c, h, phase), size), size)

    def other(c, h, phase):
        size = half >> (phase + 1)
        at = start_row(c, h, phase) + (1 - bit[orders[h][phase]]) * size
        return pl.ds(pl.multiple_of(at, size), size)

    def land(phase):
        return pl.ds(half - (half >> phase), half >> (phase + 1))

    def scatter_send(buf, rx, c, s, phase):
        return [
            send(buf.at[s, other(c, h, phase)], rx.at[s, 2 * c + h, land(phase)],
                 {"slot": across[orders[h][phase]]})
            for h in range(2)
        ]

    def gather_send(full, c, s, phase):
        return [
            send(full.at[s, block(c, h, phase + 1)], full.at[s, block(c, h, phase + 1)],
                 {"slot": across[orders[h][phase]]})
            for h in range(2)
        ]

    moving = {}

    def scatter_step(buf, rx, full, finish, c, s, phase):
        for h in range(2):
            moving[c, s][h].wait_recv()
            keep = block(c, h, phase + 1)
            got = buf[s, keep].astype(F32) + rx[s, 2 * c + h, land(phase)].astype(F32)
            if phase + 1 < bits:
                buf[s, keep] = got.astype(buf.dtype)
            else:
                finish(s, keep, got)
        if phase + 1 < bits:
            moving[c, s] = scatter_send(buf, rx, c, s, phase + 1)
        else:
            moving[c, s] = gather_send(full, c, s, bits - 1)

    def gather_step(full, c, s, phase):
        for copy in moving[c, s]:
            copy.wait_recv()
        if phase >= 0:
            moving[c, s] = gather_send(full, c, s, phase)

    tile = min(256, fdev)
    ktile = min(512, fdev)

    def columns(j, size):
        return pl.ds(pl.multiple_of(j * size, size), size)

    def encode(c, s):
        if c == 0:
            enc_in[s].wait()

        def body(j, carry):
            cols = columns(j, tile)
            part[s, rows_of(c), cols] = jnp.dot(
                acts_t[s, rows_of(c), :], encw[s, :, cols], preferred_element_type=F32
            )
            return carry

        lax.fori_loop(0, fdev // tile, body, 0)

    def forward_send(c, s):
        moving[c, s] = scatter_send(part, rxf, c, s, 0)

    def finish_forward(s, keep, total):
        feat[s, keep] = jnp.maximum(total + enc_bias[s : s + 1, :], 0.0).astype(BF16)

    def prepare():
        for t in range(layers):
            acc[t] = jnp.zeros((tokens, width), F32)
            target[t] = dec_bias[t : t + 1, :] - acts_out[t].T.astype(F32)

    def decode(c, a):
        gather_step(feat, c, a, -1)
        outs.append(local_copy(feat.at[a, rows_of(c)], feat_out.at[a, rows_of(c)]))
        for b in range(a, layers):
            p = pair_list.index((a, b))
            if c == 0:
                dec_in[p].wait()

            def body(j, carry, b=b, p=p):
                cols = columns(j, ktile)
                acc[b, rows_of(c)] += lax.dot_general(
                    feat[a, rows_of(c), cols], decw[p, :, cols],
                    (((1,), (1,)), ((), ())), preferred_element_type=F32,
                )
                return carry

            lax.fori_loop(0, fdev // ktile, body, 0)

    summing = {}

    def reconstruct(c, stage):
        own = pl.ds(pl.multiple_of(c * span + core * half, half), half)
        theirs = pl.ds(pl.multiple_of(c * span + (1 - core) * half, half), half)
        mine = pl.ds(pl.multiple_of(c * span + core * half + zpos * rows, rows), rows)
        if stage == 0:
            for t in range(layers):
                psend[c, t] = acc[t, theirs].astype(BF16)
            summing[c] = [send(psend.at[c], prx.at[c], {"feat": partner})]
        elif stage == 1:
            summing[c][0].wait_recv()
            for t in range(layers):
                total = acc[t, own] + prx[c, t].astype(F32)
                acc[t, own] = total
                zsend[c, :, t] = total.reshape(groups, rows, width).astype(zsend.dtype)
            summing[c] = [
                send(zsend.at[c, (zpos + d) % groups], zrx.at[c, d - 1], {"feat": zpeer[d]})
                for d in range(1, groups)
            ]
        elif stage == 2:
            for copy in summing[c]:
                copy.wait_recv()
            for t in range(layers):
                total = acc[t, mine]
                for d in range(1, groups):
                    total = total + zrx[c, d - 1, t].astype(F32)
                total = total + target[t, mine]
                errw[c, core, zpos, t] = total.astype(BF16).astype(errw.dtype)
            summing[c] = [
                send(errw.at[c, core, zpos], errw.at[c, core, zpos], {"feat": zpeer[d]})
                for d in range(1, groups)
            ]
        elif stage == 3:
            for copy in summing[c]:
                copy.wait_recv()
            summing[c] = [send(errw.at[c, core], errw.at[c, core], {"feat": partner})]
        elif stage == 4:
            summing[c][0].wait_recv()
            for t in range(layers):
                errb[t, rows_of(c)] = errw[c, :, :, t].reshape(span, width).astype(BF16)

    def upstream(c, a):
        def body(j, carry):
            cols = columns(j, tile)
            total = None
            for b in range(a, layers):
                term = jnp.dot(
                    errb[b, rows_of(c), :], decw[pair_list.index((a, b)), :, cols],
                    preferred_element_type=F32,
                )
                total = term if total is None else total + term
            ub[a, rows_of(c), cols] = total.astype(BF16)
            return carry

        lax.fori_loop(0, fdev // tile, body, 0)
        moving[c, a] = scatter_send(ub, rxu, c, a, 0)

    def finish_backward(s, keep, total):
        active = feat[s, keep].astype(F32) > 0.0
        delta[s, keep] = jnp.where(active, total, 0.0).astype(BF16)

    def arrive(c, s):
        gather_step(delta, c, s, -1)
        outs.append(local_copy(delta.at[s, rows_of(c)], delta_out.at[s, rows_of(c)]))

    def errors_out():
        square = jnp.zeros((1, width), F32)
        for t in range(layers):
            e = errb[t].astype(F32)
            square = square + jnp.sum(e * e, axis=0, keepdims=True)
            errt[t] = errb[t].T
        outs.append(local_copy(errt, err_out))
        ms[0] = jnp.broadcast_to(square, (8, width))
        summing["m"] = send(ms.at[0], mrx.at[0], {"slot": across[0]})

    def errors_sum(i):
        summing["m"].wait_recv()
        ms[i + 1] = ms[i] + mrx[i]
        if i + 1 < bits:
            summing["m"] = send(ms.at[i + 1], mrx.at[i + 1], {"slot": across[i + 1]})
        else:
            count = layers * tokens * width * n_slot
            mse_out[...] = jnp.sum(ms[bits, 0:1, :], axis=1, keepdims=True) / count

    up, down = range(layers), range(layers - 1, -1, -1)

    def forward_scatter(c, phase, order=up):
        for s in order:
            scatter_step(part, rxf, feat, finish_forward, c, s, phase)

    def forward_gather(c):
        for phase in range(bits - 2, -1, -1):
            for s in up:
                gather_step(feat, c, s, phase)

    def backward_scatter(c, phase):
        for s in down:
            scatter_step(ub, rxu, delta, finish_backward, c, s, phase)

    def backward_gather(c):
        for phase in range(bits - 2, -1, -1):
            for s in down:
                gather_step(delta, c, s, phase)

    for s in up:
        encode(0, s)
        forward_send(0, s)
    prepare()
    if chunks == 2:
        for s in up:
            encode(1, s)
    for phase in range(bits):
        forward_scatter(0, phase)
    if chunks == 1:
        forward_gather(0)
        for s in up:
            decode(0, s)
        for stage in range(5):
            reconstruct(0, stage)
        for s in down:
            upstream(0, s)
        errors_out()
        for phase in range(bits):
            backward_scatter(0, phase)
            errors_sum(phase)
        backward_gather(0)
        for s in down:
            arrive(0, s)
    else:
        forward_send(1, 0)
        forward_gather(0)
        for s in up[1:]:
            forward_send(1, s)
        for s in up:
            decode(0, s)
        reconstruct(0, 0)
        work = [lambda k=k: reconstruct(0, k) for k in range(1, 5)]
        work.append(lambda: upstream(0, layers - 1))
        for phase in range(bits):
            for s in up:
                scatter_step(part, rxf, feat, finish_forward, 1, s, phase)
                if work and s % 3 != 2:
                    work.pop(0)()
        while work:
            work.pop(0)()
        forward_gather(1)
        for s in down[1:]:
            upstream(0, s)
        back = [
            lambda s=s, phase=phase: scatter_step(ub, rxu, delta, finish_backward, 0, s, phase)
            for phase in range(bits) for s in down
        ]
        back += [
            lambda s=s, phase=phase: gather_step(delta, 0, s, phase)
            for phase in range(bits - 2, -1, -1) for s in down
        ]
        ahead = [lambda s=s: decode(1, s) for s in up]
        ahead += [lambda k=k: reconstruct(1, k) for k in range(5)]
        ahead += [lambda s=s: upstream(1, s) for s in down]
        for turn in "abbabbabaabaababbabb":
            steps = back if turn == "a" else ahead
            if steps:
                steps.pop(0)()
        for step in back + ahead:
            step()
        errors_out()
        for s in down:
            arrive(0, s)
        for phase in range(bits):
            backward_scatter(1, phase)
            errors_sum(phase)
        backward_gather(1)
        for s in down:
            arrive(1, s)
    for c in unsent:
        c.wait_send()
    for c in outs:
        c.wait()


def gradient_kernel(
    err_hbm, feat_hbm, acts_hbm, delta_hbm, dec_grad, enc_grad, bias_grad,
    err, feat, acts, delta, ring, in_sem, out_sem,
):
    layers, width, _ = err.shape
    fdev = feat.shape[2]
    depth, _, tile = ring.shape
    parts = out_sem.shape[1]
    loads = {}
    n_loads = 0
    for s in range(layers):
        for name, src, dst in (("err", err_hbm, err), ("feat", feat_hbm, feat)):
            loads[name, s] = pltpu.make_async_copy(src.at[s], dst.at[s], in_sem.at[n_loads])
            loads[name, s].start()
            n_loads += 1
    for s in range(layers):
        for name, src, dst in (("acts", acts_hbm, acts), ("delta", delta_hbm, delta)):
            loads[name, s] = pltpu.make_async_copy(src.at[s], dst.at[s], in_sem.at[n_loads])
            loads[name, s].start()
            n_loads += 1

    def need(name, s):
        if (name, s) in loads:
            loads.pop((name, s)).wait()

    writing = []

    def product(left, right, out):
        for j in range(fdev // tile):
            n = len(writing)
            place = n % depth
            if n >= depth:
                for c in writing[n - depth]:
                    c.wait()
            cols = pl.ds(j * tile, tile)
            ring[place] = jnp.dot(left[...], right[:, cols], preferred_element_type=F32)
            size = width // parts
            copies = []
            for k in range(parts):
                some = pl.ds(k * size, size)
                copies.append(pltpu.make_async_copy(
                    ring.at[place, some], out.at[some, cols], out_sem.at[place, k]
                ))
                copies[-1].start()
            writing.append(copies)

    for p, (a, b) in enumerate(pairs_of(layers)):
        need("feat", a)
        need("err", b)
        product(err.at[b], feat.at[a], dec_grad.at[p])
    for s in range(layers):
        need("acts", s)
        need("delta", s)
        product(acts.at[s], delta.at[s], enc_grad.at[s])
        bias_grad[s : s + 1, :] = jnp.sum(delta[s].astype(F32), axis=0, keepdims=True)
    for copies in writing[-depth:]:
        for c in copies:
            c.wait()


def gradients(err, feat, acts, delta):
    layers, width, tokens = err.shape
    fdev = feat.shape[2]
    n_pairs = len(pairs_of(layers))
    tile = min(512, fdev)
    depth, parts = 8, 2
    hbm = pl.BlockSpec(memory_space=pl.ANY)
    return pl.pallas_call(
        gradient_kernel,
        out_shape=(
            jax.ShapeDtypeStruct((n_pairs, width, fdev), F32),
            jax.ShapeDtypeStruct((layers, width, fdev), F32),
            jax.ShapeDtypeStruct((layers, fdev), F32),
        ),
        in_specs=[hbm] * 4,
        out_specs=(hbm, hbm, pl.BlockSpec(memory_space=pltpu.VMEM)),
        scratch_shapes=[
            pltpu.VMEM((layers, width, tokens), BF16),
            pltpu.VMEM((layers, tokens, fdev), BF16),
            pltpu.VMEM((layers, width, tokens), BF16),
            pltpu.VMEM((layers, tokens, fdev), BF16),
            pltpu.VMEM((depth, width, tile), F32),
            pltpu.SemaphoreType.DMA((4 * layers,)),
            pltpu.SemaphoreType.DMA((depth, parts)),
        ],
        compiler_params=pltpu.CompilerParams(vmem_limit_bytes=60 << 20),
    )(err, feat, acts, delta)


def local(n_slot, n_feat, acts_in, acts_out, enc_weight, enc_bias, dec_weight, dec_bias):
    layers, tokens, width = acts_in.shape
    fdev = enc_weight.shape[2]
    n_pairs = dec_weight.shape[0]
    chunks = chunks_of(tokens, n_slot, n_feat)
    half, groups, bits = tokens // chunks // 2, n_feat // 2, bits_of(n_slot)
    rows = half // groups
    wire = BF16 if rows % 16 == 0 else F32
    landed = half - (half >> bits)
    remote = chunks * (layers * bits * 2 * 2 * 2 + 2 * groups) + bits
    vmem = pl.BlockSpec(memory_space=pltpu.VMEM)
    hbm = pl.BlockSpec(memory_space=pl.ANY)
    acts = jnp.transpose(acts_in, (0, 2, 1))
    features, error, delta, mse = pl.pallas_call(
        functools.partial(step_kernel, n_slot, n_feat),
        out_shape=(
            jax.ShapeDtypeStruct((layers, tokens, fdev), BF16),
            jax.ShapeDtypeStruct((layers, width, tokens), BF16),
            jax.ShapeDtypeStruct((layers, tokens, fdev), BF16),
            jax.ShapeDtypeStruct((1, 1), F32),
        ),
        in_specs=[vmem, hbm, vmem, hbm, vmem, vmem],
        out_specs=(hbm, hbm, hbm, vmem),
        scratch_shapes=[
            pltpu.VMEM((layers, width, fdev), BF16),
            pltpu.VMEM((n_pairs, width, fdev), BF16),
            pltpu.VMEM((layers, tokens, width), BF16),
            pltpu.VMEM((layers, tokens, width), F32),
            pltpu.VMEM((layers, tokens, fdev), F32),
            pltpu.VMEM((layers, 2 * chunks, landed, fdev), F32),
            pltpu.VMEM((layers, tokens, fdev), BF16),
            pltpu.VMEM((layers, tokens, width), F32),
            pltpu.VMEM((chunks, layers, half, width), BF16),
            pltpu.VMEM((chunks, layers, half, width), BF16),
            pltpu.VMEM((chunks, groups, layers, rows, width), wire),
            pltpu.VMEM((chunks, groups - 1, layers, rows, width), wire),
            pltpu.VMEM((chunks, 2, groups, layers, rows, width), wire),
            pltpu.VMEM((layers, tokens, width), BF16),
            pltpu.VMEM((layers, width, tokens), BF16),
            pltpu.VMEM((layers, tokens, fdev), BF16),
            pltpu.VMEM((layers, 2 * chunks, landed, fdev), BF16),
            pltpu.VMEM((layers, tokens, fdev), BF16),
            pltpu.VMEM((bits + 1, 8, width), F32),
            pltpu.VMEM((bits, 8, width), F32),
            pltpu.SemaphoreType.DMA((layers + n_pairs + 2 * chunks * layers + 1,)),
            pltpu.SemaphoreType.DMA((remote,)),
            pltpu.SemaphoreType.DMA((remote,)),
        ],
        compiler_params=pltpu.CompilerParams(
            collective_id=0, has_side_effects=True, vmem_limit_bytes=63 << 20
        ),
    )(
        acts, enc_weight, enc_bias, jnp.transpose(dec_weight, (0, 2, 1)),
        jnp.transpose(acts_out, (0, 2, 1)), dec_bias,
    )
    dec_grads, enc_grads, bias_grads = gradients(error, features, acts, delta)
    return enc_grads, bias_grads, jnp.transpose(dec_grads, (0, 2, 1)), mse.reshape(())


def solution(mesh):
    in_specs = (
        P(None, None, "slot"),
        P(None, None, "slot"),
        P(None, "slot", "feat"),
        P(None, "feat"),
        P(None, "feat", "slot"),
        P(None, "slot"),
    )
    out_specs = (P(None, "slot", "feat"), P(None, "feat"), P(None, "feat", "slot"), P())
    body = functools.partial(local, mesh.shape["slot"], mesh.shape["feat"])
    return jax.shard_map(body, mesh=mesh, in_specs=in_specs, out_specs=out_specs, check_vma=False)
```
